32 devices in a mesh: grp: 2 (over x), col: 16 (over z, y, core).
Axes of the slice: x: 2, y: 2, z: 4, core: 2. Of those that a mesh axis runs over, the one named last changes fastest.
Arguments:
- database: int32 [256, 4096], P('col', 'grp'), parts along dimension 1, may hold values from 0 to 255
- queries: int32 [16, 256], P('grp', 'col'), parts along dimension 0, may hold values from -2147483648 to 2147483646
- key_rows: int32 [16, 8192], P('grp', 'col'), parts along dimension 0, may hold values from -2147483648 to 2147483646
- hint: int32 [4, 1024], P('grp'), parts along dimension 0, may hold values from -2147483648 to 2147483646
- assignment: int32 [32], P('grp'), parts along dimension 0, may hold values from 0 to 15, each once
Outputs:
- packed: float32 [32, 2, 1024], P(('grp', 'col')), parts along dimension 0
The draws below stay inside these ranges and needn't reach their ends.
There are 2 independent parts, one for each index of `grp`. The reference program is written for one: setup_inputs(seed, part) draws one part's arguments, and reference() takes and returns one part's arrays. A program takes and returns all parts, laid end to end along the dimension named above; each array names one. Nothing has to cross between parts.
Inputs may be any that keep to these rules, and one draw needn't show every extreme that they name: `assignment`: every unit appears in exactly one slot.
All inputs are finite; a program needn't handle non-finite values.
Results may differ from the reference program's by a relative error of at most 0.0003.
Values sent between devices are 32-bit elements; how exact they have to be, the bound alone decides.
A program may use at most 128 MiB of HBM per device.

```python
import jax
import jax.numpy as jnp
from jax import lax

CYCLE = 1024
LEVELS = 2
DIGITS = 2
CLIENTS = 8
POLYS = 2
ROWS = 2048
COLS = 256
UNITS = 16
KEY_LEN = 8192


def plant(result, key, least, top_value):
    longest = result.shape.index(max(result.shape))
    spots = []
    for shift in (0, 1):
        where = [jax.random.randint(jax.random.fold_in(key, axis), (), 0, length) for axis, length in enumerate(result.shape)]
        where[longest] = (where[longest] + shift) % result.shape[longest]
        spots.append(tuple(where))
    return result.at[spots[0]].set(least).at[spots[1]].set(top_value)


def setup_inputs(seed: int = 0, part: int = 0) -> dict:
    seeds = jax.random.split(jax.random.key(seed), 6)
    part_keys = jax.random.split(jax.random.fold_in(seeds[5], part), 6)
    database = plant(jax.random.randint(part_keys[0], (COLS, ROWS), 0, 256), jax.random.fold_in(part_keys[0], 1), 0, 255).astype(jnp.int32)
    queries = plant(jax.random.randint(part_keys[1], (CLIENTS, COLS), -2147483648, 2147483647), jax.random.fold_in(part_keys[1], 1), -2147483648, 2147483646).astype(jnp.int32)
    key_rows = plant(jax.random.randint(part_keys[2], (CLIENTS, KEY_LEN), -2147483648, 2147483647), jax.random.fold_in(part_keys[2], 1), -2147483648, 2147483646).astype(jnp.int32)
    hint = plant(jax.random.randint(part_keys[3], (POLYS, CYCLE), -2147483648, 2147483647), jax.random.fold_in(part_keys[3], 1), -2147483648, 2147483646).astype(jnp.int32)
    assignment = jax.random.permutation(part_keys[4], UNITS).astype(jnp.int32)
    return {"database": database, "queries": queries, "key_rows": key_rows, "hint": hint, "assignment": assignment}


def automorph(polynomial, galois):
    cycle_width = polynomial.shape[0]
    inverse = pow(galois, -1, 2 * cycle_width)
    source = (jnp.arange(cycle_width, dtype=jnp.int32) * inverse) % (2 * cycle_width)
    picked = jnp.take(polynomial, source % cycle_width, axis=0)
    return jnp.where(source < cycle_width, picked, -picked)


def toeplitz(key_poly):
    cycle_width = key_poly.shape[0]
    shifted = jnp.concatenate([-key_poly[1:], key_poly, -key_poly[:1]])
    tiled_rows = jnp.tile(shifted, cycle_width)[: cycle_width * (2 * cycle_width - 1)]
    return tiled_rows.reshape(cycle_width, 2 * cycle_width - 1)[:, cycle_width - 1:2 * cycle_width - 1]


def switch_section(mask_poly, value_poly, section_keys, galois):
    cycle_width = mask_poly.shape[0]
    rotated_mask = automorph(mask_poly, galois)
    rotated_value = automorph(value_poly, galois)
    switched = jnp.zeros((2 * cycle_width,), jnp.int32)
    for digit_index in range(section_keys.shape[0]):
        digit_row = jnp.bitwise_and(jnp.right_shift(rotated_mask, 16 * digit_index), 65535)
        matrix = jnp.concatenate([toeplitz(section_keys[digit_index, 0]), toeplitz(section_keys[digit_index, 1])], axis=1)
        switched = switched + jnp.dot(digit_row[None, :], matrix, preferred_element_type=jnp.int32)[0]
    return mask_poly + switched[:cycle_width], value_poly + rotated_value + switched[cycle_width:]


def pack_unit(mask_poly, value_poly, key_row):
    cycle_width = mask_poly.shape[0]
    section_table = key_row.reshape(LEVELS, DIGITS, 2, cycle_width)
    for section_index in range(LEVELS):
        galois = cycle_width // (2 ** section_index) + 1
        mask_poly, value_poly = switch_section(mask_poly, value_poly, section_table[section_index], galois)
    return jnp.stack([mask_poly, value_poly])


def reference(database, queries, key_rows, hint, assignment):
    answers = jnp.dot(queries, database, preferred_element_type=jnp.int32)
    unit_rows = answers.reshape(CLIENTS * POLYS, CYCLE)

    def pack_one(unit_index):
        client = unit_index // POLYS
        poly_index = unit_index % POLYS
        mask_poly = lax.dynamic_index_in_dim(hint, poly_index, 0, keepdims=False)
        value_poly = lax.dynamic_index_in_dim(unit_rows, unit_index, 0, keepdims=False)
        key_row = lax.dynamic_index_in_dim(key_rows, client, 0, keepdims=False)
        return pack_unit(mask_poly, value_poly, key_row)

    packed_words = lax.map(pack_one, assignment)
    return packed_words.astype(jnp.float32) * (2.0 ** -32)
```

```python
import functools

import jax
import jax.numpy as jnp
from jax import lax
from jax.experimental import pallas as pl
from jax.experimental.pallas import tpu as pltpu
from jax.sharding import PartitionSpec as P

LEVELS = 2
DIGITS = 2
LANES = 128
WORD_BYTES = 4
DIGIT_BYTES = WORD_BYTES // DIGITS


def iota(shape, axis):
    return lax.broadcasted_iota(jnp.int32, shape, axis)


def byte_of(words, index):
    return jnp.bitwise_and(jnp.right_shift(words, 8 * index), 255).astype(jnp.float32)


def shifted(poly, amount):
    rows = poly.shape[0]
    amount = amount % (2 * rows * LANES)
    negate, turn = divmod(amount // LANES, rows)
    moved = poly
    if turn:
        moved = pltpu.roll(poly, turn, 0)
        moved = jnp.where(iota(poly.shape, 0) >= turn, moved, -moved)
    return -moved if negate else moved


def automorph(poly, level):
    step = poly.shape[0] * LANES >> level
    period = 2 << level
    residue = jnp.bitwise_and(iota(poly.shape, 1), period - 1)
    out = poly
    for m in range(1, period):
        out = jnp.where(residue == m, shifted(poly, step * m), out)
    return out


def fill_toeplitz(word_poly, toeplitz):
    rows = word_poly.shape[0]
    square = (LANES, LANES)
    ahead = iota(square, 1) >= iota(square, 0)

    def turned(q):
        row = jnp.broadcast_to(word_poly[q : q + 1], square)
        return pltpu.roll(row, 0, 1, stride=1, stride_axis=0)

    before = turned(rows - 1)
    for q in range(rows):
        here = turned(q)
        words = jnp.where(ahead, here, before)
        for t in range(DIGITS):
            for a in range(DIGIT_BYTES):
                part = byte_of(words, t * DIGIT_BYTES + a)
                if q == 0:
                    part = jnp.where(ahead, part, -part)
                toeplitz[t, a * LANES : (a + 1) * LANES, q * LANES : (q + 1) * LANES] = part.astype(
                    jnp.bfloat16
                )
        before = here


def key_side(keys):
    zero = jnp.zeros(keys[0].shape, jnp.float32)
    columns = []
    for a in range(DIGIT_BYTES):
        blocks = [byte_of(k, s - a) if s >= a else zero for s in range(WORD_BYTES) for k in keys]
        columns.append(jnp.concatenate(blocks, axis=0))
    return jnp.concatenate(columns, axis=1).astype(jnp.bfloat16)


def switch(toeplitz, key_polys, rows):
    cycle = rows * LANES
    products = [
        jnp.dot(key_side(key_polys[t]), toeplitz[t], preferred_element_type=jnp.float32).astype(jnp.int32)
        for t in range(DIGITS)
    ]
    sums = []
    for p in range(2):
        words = jnp.zeros((rows, cycle), jnp.int32)
        for s in range(WORD_BYTES):
            at = (s * 2 + p) * rows
            total = products[0][at : at + rows]
            for t in range(1, DIGITS):
                total = total + products[t][at : at + rows]
            words = words + jnp.left_shift(total, 8 * s)
        out = jnp.zeros((rows, LANES), jnp.int32)
        for q in range(rows):
            out = out + shifted(words[:, q * LANES : (q + 1) * LANES], q * LANES)
        sums.append(out)
    return sums


def kernel(
    n, slots, share, assign, database, queries, keys, hint, out,
    part, unit_part, unit_keys, unit_masks, ans_send, key_send, ans_recv, key_recv, key_words, toeplitz,
    ans_sent, key_sent, ans_got, key_got,
):
    me = lax.axis_index("col")
    clients, columns = queries.shape
    polys, cycle = hint.shape
    rows = cycle // LANES
    key_rows = unit_keys.shape[1]
    barrier = pltpu.get_barrier_semaphore()

    def greet(i, carry):
        pl.semaphore_signal(barrier, inc=1, device_id={"col": lax.rem(me + i, n)})
        return carry

    lax.fori_loop(1, n, greet, 0)

    lane_owner = iota((clients, LANES), 1) // (LANES // share)
    for j in range(key_rows):
        tile = keys[:, j * LANES : (j + 1) * LANES]
        if share > 1:
            tile = jnp.where(lane_owner == lax.rem(me, share), tile, 0)
        for c in range(clients):
            for p in range(polys):
                unit_keys[c * polys + p, j : j + 1, :] = tile[c : c + 1]

    for p in range(polys):
        for q in range(rows):
            row = hint[p : p + 1, q * LANES : (q + 1) * LANES]
            for c in range(clients):
                unit_masks[c * polys + p, q : q + 1, :] = row

    query_words = queries[...]
    query_bytes = jnp.concatenate([byte_of(query_words, b) for b in range(WORD_BYTES)], axis=0)
    products = jnp.dot(
        query_bytes.astype(jnp.bfloat16),
        database[...].astype(jnp.float32).astype(jnp.bfloat16),
        preferred_element_type=jnp.float32,
    ).astype(jnp.int32)
    partial = products[:clients]
    for b in range(1, WORD_BYTES):
        partial = partial + jnp.left_shift(products[b * clients : (b + 1) * clients], 8 * b)
    for j in range(polys * rows):
        part[j * clients : (j + 1) * clients, :] = partial[:, j * LANES : (j + 1) * LANES]

    for c in range(clients):
        for p in range(polys):
            unit_part[c * polys + p] = part[pl.ds(p * rows * clients + c, rows, stride=clients), :]

    def stage_into(ans, key, at, owner):
        for k in range(slots):
            unit = assign[owner * slots + k]
            ans[at, k * rows : (k + 1) * rows, :] = unit_part[unit]
            key[at, k * key_rows : (k + 1) * key_rows, :] = unit_keys[unit]

    def stage(i, carry):
        owner = lax.rem(me + i, n)
        stage_into(ans_send, key_send, owner, owner)
        return carry

    lax.fori_loop(1, n, stage, 0)
    stage_into(ans_recv, key_recv, me, me)

    pl.semaphore_wait(barrier, n - 1)

    def key_copy(there, slot):
        return pltpu.make_async_remote_copy(
            src_ref=key_send.at[there],
            dst_ref=key_recv.at[slot],
            send_sem=key_sent.at[there],
            recv_sem=key_got.at[slot],
            device_id={"col": there},
        )

    def ans_copy(there, slot):
        return pltpu.make_async_remote_copy(
            src_ref=ans_send.at[there],
            dst_ref=ans_recv.at[slot],
            send_sem=ans_sent.at[there],
            recv_sem=ans_got.at[slot],
            device_id={"col": there},
        )

    def send_keys(i, carry):
        key_copy(lax.rem(me + i, n), me).start()
        return carry

    def send_answers(i, carry):
        ans_copy(lax.rem(me + i, n), me).start()
        return carry

    def got_keys(i, carry):
        there = lax.rem(me + i, n)
        key_copy(there, there).wait_recv()
        return carry

    def got_answers(i, carry):
        there = lax.rem(me + i, n)
        ans_copy(there, there).wait_recv()
        return carry

    def sent(i, carry):
        there = lax.rem(me + i, n)
        key_copy(there, me).wait_send()
        ans_copy(there, me).wait_send()
        return carry

    lax.fori_loop(1, n, send_keys, 0)
    lax.fori_loop(1, n, send_answers, 0)

    switched = []
    for k in range(slots):
        mask = unit_masks[assign[me * slots + k]]
        fill_toeplitz(automorph(mask, 0), toeplitz)
        if k == 0:
            lax.fori_loop(1, n, got_keys, 0)
        for j in range(n // share):
            block = key_recv[j * share, k * key_rows : (k + 1) * key_rows, :]
            for h in range(1, share):
                block = block + key_recv[j * share + h, k * key_rows : (k + 1) * key_rows, :]
            key_words[j * key_rows : (j + 1) * key_rows, :] = block
        added = []
        for level in range(LEVELS):
            if level:
                fill_toeplitz(automorph(mask, level), toeplitz)

            def key_poly(t, p):
                at = ((level * DIGITS + t) * 2 + p) * rows
                return key_words[at : at + rows, :]

            to_mask, to_value = switch(
                toeplitz, [[key_poly(t, p) for p in range(2)] for t in range(DIGITS)], rows
            )
            mask = mask + to_mask
            added.append(to_value)
        switched.append((mask, added))

    lax.fori_loop(1, n, got_answers, 0)
    for k, (mask, added) in enumerate(switched):
        value = ans_recv[0, k * rows : (k + 1) * rows, :]
        for j in range(1, n):
            value = value + ans_recv[j, k * rows : (k + 1) * rows, :]
        for level in range(LEVELS):
            value = value + automorph(value, level) + added[level]
        for index, words in enumerate((mask, value)):
            scaled = words.astype(jnp.float32) * 2.0 ** (-32)
            for q in range(rows):
                out[k, index : index + 1, q * LANES : (q + 1) * LANES] = scaled[q : q + 1]
    lax.fori_loop(1, n, sent, 0)


def solution(mesh):
    n = mesh.shape["col"]

    def on_device(database, queries, key_rows, hint, assignment):
        clients = queries.shape[0]
        polys, cycle = hint.shape
        rows = cycle // LANES
        slots = assignment.shape[0] // n
        width = key_rows.shape[1]
        share = max(1, LANES // width)
        if share > 1:
            key_rows = jnp.tile(key_rows, (1, share))
        tiles = key_rows.shape[1] // LANES
        vmem = pl.BlockSpec(memory_space=pltpu.VMEM)
        return pl.pallas_call(
            functools.partial(kernel, n, slots, share),
            out_shape=jax.ShapeDtypeStruct((slots, 2, cycle), jnp.float32),
            in_specs=[pl.BlockSpec(memory_space=pltpu.SMEM), vmem, vmem, vmem, vmem],
            out_specs=vmem,
            scratch_shapes=[
                pltpu.VMEM((polys * rows * clients, LANES), jnp.int32),
                pltpu.VMEM((polys * clients, rows, LANES), jnp.int32),
                pltpu.VMEM((polys * clients, tiles, LANES), jnp.int32),
                pltpu.VMEM((polys * clients, rows, LANES), jnp.int32),
                pltpu.VMEM((n, slots * rows, LANES), jnp.int32),
                pltpu.VMEM((n, slots * tiles, LANES), jnp.int32),
                pltpu.VMEM((n, slots * rows, LANES), jnp.int32),
                pltpu.VMEM((n, slots * tiles, LANES), jnp.int32),
                pltpu.VMEM((n // share * tiles, LANES), jnp.int32),
                pltpu.VMEM((DIGITS, DIGIT_BYTES * LANES, cycle), jnp.bfloat16),
                pltpu.SemaphoreType.DMA((n,)),
                pltpu.SemaphoreType.DMA((n,)),
                pltpu.SemaphoreType.DMA((n,)),
                pltpu.SemaphoreType.DMA((n,)),
            ],
            compiler_params=pltpu.CompilerParams(collective_id=0, has_side_effects=True),
        )(assignment, database, queries, key_rows, hint)

    placed = (P("col", "grp"), P("grp", "col"), P("grp", "col"), P("grp", None), P("grp"))
    return jax.shard_map(
        on_device,
        mesh=mesh,
        in_specs=placed,
        out_specs=P(("grp", "col"), None, None),
        check_vma=False,
    )
```

```python
import functools

import jax
import jax.numpy as jnp
from jax import lax
from jax.experimental import pallas as pl
from jax.experimental.pallas import tpu as pltpu
from jax.sharding import PartitionSpec as P

LEVELS = 2
DIGITS = 2
LANES = 128
WORD_BYTES = 4
DIGIT_BYTES = WORD_BYTES // DIGITS


def iota(shape, axis):
    return lax.broadcasted_iota(jnp.int32, shape, axis)


def byte_of(words, index):
    return jnp.bitwise_and(jnp.right_shift(words, 8 * index), 255).astype(jnp.float32)


def shifted(poly, amount):
    rows = poly.shape[0]
    amount = amount % (2 * rows * LANES)
    negate, turn = divmod(amount // LANES, rows)
    moved = poly
    if turn:
        moved = pltpu.roll(poly, turn, 0)
        moved = jnp.where(iota(poly.shape, 0) >= turn, moved, -moved)
    return -moved if negate else moved


def automorph(poly, level):
    step = poly.shape[0] * LANES >> level
    period = 2 << level
    residue = jnp.bitwise_and(iota(poly.shape, 1), period - 1)
    out = poly
    for m in range(1, period):
        out = jnp.where(residue == m, shifted(poly, step * m), out)
    return out


def fill_toeplitz(word_poly, toeplitz):
    rows = word_poly.shape[0]
    square = (LANES, LANES)
    ahead = iota(square, 1) >= iota(square, 0)

    def turned(q):
        row = jnp.broadcast_to(word_poly[q : q + 1], square)
        return pltpu.roll(row, 0, 1, stride=1, stride_axis=0)

    before = turned(rows - 1)
    for q in range(rows):
        here = turned(q)
        words = jnp.where(ahead, here, before)
        for t in range(DIGITS):
            for a in range(DIGIT_BYTES):
                part = byte_of(words, t * DIGIT_BYTES + a)
                if q == 0:
                    part = jnp.where(ahead, part, -part)
                toeplitz[t, a * LANES : (a + 1) * LANES, q * LANES : (q + 1) * LANES] = part.astype(
                    jnp.bfloat16
                )
        before = here


def key_side(keys):
    zero = jnp.zeros(keys[0].shape, jnp.float32)
    columns = []
    for a in range(DIGIT_BYTES):
        blocks = [byte_of(k, s - a) if s >= a else zero for s in range(WORD_BYTES) for k in keys]
        columns.append(jnp.concatenate(blocks, axis=0))
    return jnp.concatenate(columns, axis=1).astype(jnp.bfloat16)


def switch(toeplitz, key_polys, rows):
    cycle = rows * LANES
    products = [
        jnp.dot(key_side(key_polys[t]), toeplitz[t], preferred_element_type=jnp.float32).astype(jnp.int32)
        for t in range(DIGITS)
    ]
    sums = []
    for p in range(2):
        words = jnp.zeros((rows, cycle), jnp.int32)
        for s in range(WORD_BYTES):
            at = (s * 2 + p) * rows
            total = products[0][at : at + rows]
            for t in range(1, DIGITS):
                total = total + products[t][at : at + rows]
            words = words + jnp.left_shift(total, 8 * s)
        out = jnp.zeros((rows, LANES), jnp.int32)
        for q in range(rows):
            out = out + shifted(words[:, q * LANES : (q + 1) * LANES], q * LANES)
        sums.append(out)
    return sums


def kernel(
    n, slots, share, assign_hbm, database_hbm, queries_hbm, keys_hbm, hint_hbm, out,
    assign, database, queries, keys, hint, loaded, part, unit_part, unit_keys, unit_masks, ans_send, key_send, ans_recv, key_recv, key_words, toeplitz,
    ans_sent, key_sent, ans_got, key_got,
):
    me = lax.axis_index("col")
    clients, columns = queries.shape
    polys, cycle = hint.shape
    rows = cycle // LANES
    key_rows = unit_keys.shape[1]
    barrier = pltpu.get_barrier_semaphore()

    def greet(i, carry):
        pl.semaphore_signal(barrier, inc=1, device_id={"col": lax.rem(me + i, n)})
        return carry

    lax.fori_loop(1, n, greet, 0)

    loads = [
        pltpu.make_async_copy(source, target, loaded.at[i])
        for i, (source, target) in enumerate(
            (
                (keys_hbm, keys),
                (hint_hbm, hint),
                (assign_hbm, assign),
                (queries_hbm, queries),
                (database_hbm, database),
            )
        )
    ]
    for load in loads:
        load.start()

    loads[0].wait()
    lane_owner = iota((clients, LANES), 1) // (LANES // share)
    for j in range(key_rows):
        tile = keys[:, j * LANES : (j + 1) * LANES]
        if share > 1:
            tile = jnp.where(lane_owner == lax.rem(me, share), tile, 0)
        for c in range(clients):
            for p in range(polys):
                unit_keys[c * polys + p, j : j + 1, :] = tile[c : c + 1]

    loads[1].wait()
    for p in range(polys):
        for q in range(rows):
            row = hint[p : p + 1, q * LANES : (q + 1) * LANES]
            for c in range(clients):
                unit_masks[c * polys + p, q : q + 1, :] = row

    for load in loads[2:]:
        load.wait()
    query_words = queries[...]
    query_bytes = jnp.concatenate([byte_of(query_words, b) for b in range(WORD_BYTES)], axis=0)
    products = jnp.dot(
        query_bytes.astype(jnp.bfloat16),
        database[...].astype(jnp.float32).astype(jnp.bfloat16),
        preferred_element_type=jnp.float32,
    ).astype(jnp.int32)
    partial = products[:clients]
    for b in range(1, WORD_BYTES):
        partial = partial + jnp.left_shift(products[b * clients : (b + 1) * clients], 8 * b)
    for j in range(polys * rows):
        part[j * clients : (j + 1) * clients, :] = partial[:, j * LANES : (j + 1) * LANES]

    for c in range(clients):
        for p in range(polys):
            unit_part[c * polys + p] = part[pl.ds(p * rows * clients + c, rows, stride=clients), :]

    def stage_into(ans, key, at, owner):
        for k in range(slots):
            unit = assign[owner * slots + k]
            ans[at, k * rows : (k + 1) * rows, :] = unit_part[unit]
            key[at, k * key_rows : (k + 1) * key_rows, :] = unit_keys[unit]

    def stage(i, carry):
        owner = lax.rem(me + i, n)
        stage_into(ans_send, key_send, owner, owner)
        return carry

    lax.fori_loop(1, n, stage, 0)
    stage_into(ans_recv, key_recv, me, me)

    pl.semaphore_wait(barrier, n - 1)

    def key_copy(there, slot):
        return pltpu.make_async_remote_copy(
            src_ref=key_send.at[there],
            dst_ref=key_recv.at[slot],
            send_sem=key_sent.at[there],
            recv_sem=key_got.at[slot],
            device_id={"col": there},
        )

    def ans_copy(there, slot):
        return pltpu.make_async_remote_copy(
            src_ref=ans_send.at[there],
            dst_ref=ans_recv.at[slot],
            send_sem=ans_sent.at[there],
            recv_sem=ans_got.at[slot],
            device_id={"col": there},
        )

    def send_keys(i, carry):
        key_copy(lax.rem(me + i, n), me).start()
        return carry

    def send_answers(i, carry):
        ans_copy(lax.rem(me + i, n), me).start()
        return carry

    def got_keys(i, carry):
        there = lax.rem(me + i, n)
        key_copy(there, there).wait_recv()
        return carry

    def got_answers(i, carry):
        there = lax.rem(me + i, n)
        ans_copy(there, there).wait_recv()
        return carry

    def sent(i, carry):
        there = lax.rem(me + i, n)
        key_copy(there, me).wait_send()
        ans_copy(there, me).wait_send()
        return carry

    lax.fori_loop(1, n, send_keys, 0)
    lax.fori_loop(1, n, send_answers, 0)

    switched = []
    for k in range(slots):
        mask = unit_masks[assign[me * slots + k]]
        fill_toeplitz(automorph(mask, 0), toeplitz)
        if k == 0:
            lax.fori_loop(1, n, got_keys, 0)
        for j in range(n // share):
            block = key_recv[j * share, k * key_rows : (k + 1) * key_rows, :]
            for h in range(1, share):
                block = block + key_recv[j * share + h, k * key_rows : (k + 1) * key_rows, :]
            key_words[j * key_rows : (j + 1) * key_rows, :] = block
        added = []
        for level in range(LEVELS):
            if level:
                fill_toeplitz(automorph(mask, level), toeplitz)

            def key_poly(t, p):
                at = ((level * DIGITS + t) * 2 + p) * rows
                return key_words[at : at + rows, :]

            to_mask, to_value = switch(
                toeplitz, [[key_poly(t, p) for p in range(2)] for t in range(DIGITS)], rows
            )
            mask = mask + to_mask
            added.append(to_value)
        switched.append((mask, added))

    lax.fori_loop(1, n, got_answers, 0)
    for k, (mask, added) in enumerate(switched):
        value = ans_recv[0, k * rows : (k + 1) * rows, :]
        for j in range(1, n):
            value = value + ans_recv[j, k * rows : (k + 1) * rows, :]
        for level in range(LEVELS):
            value = value + automorph(value, level) + added[level]
        for index, words in enumerate((mask, value)):
            scaled = words.astype(jnp.float32) * 2.0 ** (-32)
            for q in range(rows):
                out[k, index : index + 1, q * LANES : (q + 1) * LANES] = scaled[q : q + 1]
    lax.fori_loop(1, n, sent, 0)


def solution(mesh):
    n = mesh.shape["col"]

    def on_device(database, queries, key_rows, hint, assignment):
        clients = queries.shape[0]
        polys, cycle = hint.shape
        rows = cycle // LANES
        slots = assignment.shape[0] // n
        width = key_rows.shape[1]
        share = max(1, LANES // width)
        if share > 1:
            key_rows = jnp.tile(key_rows, (1, share))
        tiles = key_rows.shape[1] // LANES
        place = pl.BlockSpec(memory_space=pltpu.HBM)
        return pl.pallas_call(
            functools.partial(kernel, n, slots, share),
            out_shape=pltpu.VMEM((slots, 2, cycle), jnp.float32),
            in_specs=[place] * 5,
            out_specs=pl.BlockSpec(memory_space=pltpu.VMEM),
            scratch_shapes=[
                pltpu.SMEM(assignment.shape, jnp.int32),
                pltpu.VMEM(database.shape, jnp.int32),
                pltpu.VMEM(queries.shape, jnp.int32),
                pltpu.VMEM(key_rows.shape, jnp.int32),
                pltpu.VMEM(hint.shape, jnp.int32),
                pltpu.SemaphoreType.DMA((5,)),
                pltpu.VMEM((polys * rows * clients, LANES), jnp.int32),
                pltpu.VMEM((polys * clients, rows, LANES), jnp.int32),
                pltpu.VMEM((polys * clients, tiles, LANES), jnp.int32),
                pltpu.VMEM((polys * clients, rows, LANES), jnp.int32),
                pltpu.VMEM((n, slots * rows, LANES), jnp.int32),
                pltpu.VMEM((n, slots * tiles, LANES), jnp.int32),
                pltpu.VMEM((n, slots * rows, LANES), jnp.int32),
                pltpu.VMEM((n, slots * tiles, LANES), jnp.int32),
                pltpu.VMEM((n // share * tiles, LANES), jnp.int32),
                pltpu.VMEM((DIGITS, DIGIT_BYTES * LANES, cycle), jnp.bfloat16),
                pltpu.SemaphoreType.DMA((n,)),
                pltpu.SemaphoreType.DMA((n,)),
                pltpu.SemaphoreType.DMA((n,)),
                pltpu.SemaphoreType.DMA((n,)),
            ],
            compiler_params=pltpu.CompilerParams(
                collective_id=0, has_side_effects=True
            ),
        )(*(pltpu.with_memory_space_constraint(x, pltpu.HBM) for x in (assignment, database, queries, key_rows, hint)))

    placed = (P("col", "grp"), P("grp", "col"), P("grp", "col"), P("grp", None), P("grp"))
    return jax.shard_map(
        on_device,
        mesh=mesh,
        in_specs=placed,
        out_specs=P(("grp", "col"), None, None),
        check_vma=False,
    )
```

```python
import functools

import jax
import jax.numpy as jnp
from jax import lax
from jax.experimental import pallas as pl
from jax.experimental.pallas import tpu as pltpu
from jax.sharding import PartitionSpec as P

LEVELS = 2
DIGITS = 2
LANES = 128
WORD_BYTES = 4
DIGIT_BYTES = WORD_BYTES // DIGITS


def iota(shape, axis):
    return lax.broadcasted_iota(jnp.int32, shape, axis)


def byte_of(words, index):
    return jnp.bitwise_and(jnp.right_shift(words, 8 * index), 255).astype(jnp.float32)


def shifted(poly, amount):
    rows = poly.shape[0]
    amount = amount % (2 * rows * LANES)
    negate, turn = divmod(amount // LANES, rows)
    moved = poly
    if turn:
        moved = pltpu.roll(poly, turn, 0)
        moved = jnp.where(iota(poly.shape, 0) >= turn, moved, -moved)
    return -moved if negate else moved


def automorph(poly, level):
    step = poly.shape[0] * LANES >> level
    period = 2 << level
    residue = jnp.bitwise_and(iota(poly.shape, 1), period - 1)
    out = poly
    for m in range(1, period):
        out = jnp.where(residue == m, shifted(poly, step * m), out)
    return out


def fill_toeplitz(word_poly, toeplitz):
    rows = word_poly.shape[0]
    square = (LANES, LANES)
    ahead = iota(square, 1) >= iota(square, 0)

    def turned(q):
        row = jnp.broadcast_to(word_poly[q : q + 1], square)
        return pltpu.roll(row, 0, 1, stride=1, stride_axis=0)

    before = turned(rows - 1)
    for q in range(rows):
        here = turned(q)
        words = jnp.where(ahead, here, before)
        for t in range(DIGITS):
            for a in range(DIGIT_BYTES):
                part = byte_of(words, t * DIGIT_BYTES + a)
                if q == 0:
                    part = jnp.where(ahead, part, -part)
                toeplitz[t, a * LANES : (a + 1) * LANES, q * LANES : (q + 1) * LANES] = part.astype(
                    jnp.bfloat16
                )
        before = here


def key_side(keys):
    zero = jnp.zeros(keys[0].shape, jnp.float32)
    columns = []
    for a in range(DIGIT_BYTES):
        blocks = [byte_of(k, s - a) if s >= a else zero for s in range(WORD_BYTES) for k in keys]
        columns.append(jnp.concatenate(blocks, axis=0))
    return jnp.concatenate(columns, axis=1).astype(jnp.bfloat16)


def switch(toeplitz, key_polys, rows):
    cycle = rows * LANES
    products = [
        jnp.dot(key_side(key_polys[t]), toeplitz[t], preferred_element_type=jnp.float32).astype(jnp.int32)
        for t in range(DIGITS)
    ]
    sums = []
    for p in range(2):
        words = jnp.zeros((rows, cycle), jnp.int32)
        for s in range(WORD_BYTES):
            at = (s * 2 + p) * rows
            total = products[0][at : at + rows]
            for t in range(1, DIGITS):
                total = total + products[t][at : at + rows]
            words = words + jnp.left_shift(total, 8 * s)
        out = jnp.zeros((rows, LANES), jnp.int32)
        for q in range(rows):
            out = out + shifted(words[:, q * LANES : (q + 1) * LANES], q * LANES)
        sums.append(out)
    return sums


def kernel(
    n, slots, share, assign_hbm, database_hbm, queries_hbm, keys_hbm, hint_hbm, out,
    assign, database, queries, keys, hint, loaded, part, unit_part, unit_keys, unit_masks, ans_send, key_send, ans_recv, key_recv, key_words, toeplitz,
    ans_sent, key_sent, ans_got, key_got,
):
    me = lax.axis_index("col")
    clients, columns = queries.shape
    polys, cycle = hint.shape
    rows = cycle // LANES
    key_rows = unit_keys.shape[1]
    barrier = pltpu.get_barrier_semaphore()

    def greet(i, carry):
        pl.semaphore_signal(barrier, inc=1, device_id={"col": lax.rem(me + i, n)})
        return carry

    lax.fori_loop(1, n, greet, 0)

    loads = [
        pltpu.make_async_copy(source, target, loaded.at[i])
        for i, (source, target) in enumerate(
            (
                (keys_hbm, keys),
                (hint_hbm, hint),
                (assign_hbm, assign),
                (queries_hbm, queries),
                (database_hbm, database),
            )
        )
    ]
    for load in loads:
        load.start()

    loads[0].wait()
    lane_owner = iota((clients, LANES), 1) // (LANES // share)
    for j in range(key_rows):
        tile = keys[:, j * LANES : (j + 1) * LANES]
        if share > 1:
            tile = jnp.where(lane_owner == lax.rem(me, share), tile, 0)
        for c in range(clients):
            for p in range(polys):
                unit_keys[c * polys + p, j : j + 1, :] = tile[c : c + 1]

    loads[1].wait()
    for p in range(polys):
        for q in range(rows):
            row = hint[p : p + 1, q * LANES : (q + 1) * LANES]
            for c in range(clients):
                unit_masks[c * polys + p, q : q + 1, :] = row

    for load in loads[2:]:
        load.wait()
    query_words = queries[...]
    query_bytes = jnp.concatenate([byte_of(query_words, b) for b in range(WORD_BYTES)], axis=0)
    products = jnp.dot(
        query_bytes.astype(jnp.bfloat16),
        database[...].astype(jnp.float32).astype(jnp.bfloat16),
        preferred_element_type=jnp.float32,
    ).astype(jnp.int32)
    partial = products[:clients]
    for b in range(1, WORD_BYTES):
        partial = partial + jnp.left_shift(products[b * clients : (b + 1) * clients], 8 * b)
    for j in range(polys * rows):
        part[j * clients : (j + 1) * clients, :] = partial[:, j * LANES : (j + 1) * LANES]

    for c in range(clients):
        for p in range(polys):
            unit_part[c * polys + p] = part[pl.ds(p * rows * clients + c, rows, stride=clients), :]

    def stage_into(ans, key, at, owner):
        for k in range(slots):
            unit = assign[owner * slots + k]
            ans[at, k * rows : (k + 1) * rows, :] = unit_part[unit]
            key[at, k * key_rows : (k + 1) * key_rows, :] = unit_keys[unit]

    def stage(i, carry):
        owner = lax.rem(me + i, n)
        stage_into(ans_send, key_send, owner, owner)
        return carry

    lax.fori_loop(1, n, stage, 0)
    stage_into(ans_recv, key_recv, me, me)

    pl.semaphore_wait(barrier, n - 1)

    def remote(source, target, there, sent, got):
        return pltpu.make_async_remote_copy(
            src_ref=source.at[there],
            dst_ref=target.at[me],
            send_sem=sent,
            recv_sem=got,
            device_id={"col": there},
        )

    def send_keys(i, carry):
        remote(key_send, key_recv, lax.rem(me + i, n), key_sent, key_got).start()
        return carry

    def send_answers(i, carry):
        remote(ans_send, ans_recv, lax.rem(me + i, n), ans_sent, ans_got).start()
        return carry

    def wait_all(buffer, semaphore):
        blocks = buffer.at[pl.ds(0, n - 1)]
        pltpu.make_async_copy(blocks, blocks, semaphore).wait()

    lax.fori_loop(1, n, send_keys, 0)
    lax.fori_loop(1, n, send_answers, 0)

    switched = []
    for k in range(slots):
        mask = unit_masks[assign[me * slots + k]]
        fill_toeplitz(automorph(mask, 0), toeplitz)
        if k == 0:
            wait_all(key_recv, key_got)
        for j in range(n // share):
            block = key_recv[j * share, k * key_rows : (k + 1) * key_rows, :]
            for h in range(1, share):
                block = block + key_recv[j * share + h, k * key_rows : (k + 1) * key_rows, :]
            key_words[j * key_rows : (j + 1) * key_rows, :] = block
        added = []
        for level in range(LEVELS):
            if level:
                fill_toeplitz(automorph(mask, level), toeplitz)

            def key_poly(t, p):
                at = ((level * DIGITS + t) * 2 + p) * rows
                return key_words[at : at + rows, :]

            to_mask, to_value = switch(
                toeplitz, [[key_poly(t, p) for p in range(2)] for t in range(DIGITS)], rows
            )
            mask = mask + to_mask
            added.append(to_value)
        switched.append((mask, added))

    wait_all(ans_recv, ans_got)
    for k, (mask, added) in enumerate(switched):
        value = ans_recv[0, k * rows : (k + 1) * rows, :]
        for j in range(1, n):
            value = value + ans_recv[j, k * rows : (k + 1) * rows, :]
        for level in range(LEVELS):
            value = value + automorph(value, level) + added[level]
        for index, words in enumerate((mask, value)):
            scaled = words.astype(jnp.float32) * 2.0 ** (-32)
            for q in range(rows):
                out[k, index : index + 1, q * LANES : (q + 1) * LANES] = scaled[q : q + 1]
    wait_all(key_send, key_sent)
    wait_all(ans_send, ans_sent)


def solution(mesh):
    n = mesh.shape["col"]

    def on_device(database, queries, key_rows, hint, assignment):
        clients = queries.shape[0]
        polys, cycle = hint.shape
        rows = cycle // LANES
        slots = assignment.shape[0] // n
        width = key_rows.shape[1]
        share = max(1, LANES // width)
        if share > 1:
            key_rows = jnp.tile(key_rows, (1, share))
        tiles = key_rows.shape[1] // LANES
        place = pl.BlockSpec(memory_space=pltpu.HBM)
        return pl.pallas_call(
            functools.partial(kernel, n, slots, share),
            out_shape=pltpu.VMEM((slots, 2, cycle), jnp.float32),
            in_specs=[place] * 5,
            out_specs=pl.BlockSpec(memory_space=pltpu.VMEM),
            scratch_shapes=[
                pltpu.SMEM(assignment.shape, jnp.int32),
                pltpu.VMEM(database.shape, jnp.int32),
                pltpu.VMEM(queries.shape, jnp.int32),
                pltpu.VMEM(key_rows.shape, jnp.int32),
                pltpu.VMEM(hint.shape, jnp.int32),
                pltpu.SemaphoreType.DMA((5,)),
                pltpu.VMEM((polys * rows * clients, LANES), jnp.int32),
                pltpu.VMEM((polys * clients, rows, LANES), jnp.int32),
                pltpu.VMEM((polys * clients, tiles, LANES), jnp.int32),
                pltpu.VMEM((polys * clients, rows, LANES), jnp.int32),
                pltpu.VMEM((n, slots * rows, LANES), jnp.int32),
                pltpu.VMEM((n, slots * tiles, LANES), jnp.int32),
                pltpu.VMEM((n, slots * rows, LANES), jnp.int32),
                pltpu.VMEM((n, slots * tiles, LANES), jnp.int32),
                pltpu.VMEM((n // share * tiles, LANES), jnp.int32),
                pltpu.VMEM((DIGITS, DIGIT_BYTES * LANES, cycle), jnp.bfloat16),
                pltpu.SemaphoreType.DMA,
                pltpu.SemaphoreType.DMA,
                pltpu.SemaphoreType.DMA,
                pltpu.SemaphoreType.DMA,
            ],
            compiler_params=pltpu.CompilerParams(
                collective_id=0, has_side_effects=True
            ),
        )(*(pltpu.with_memory_space_constraint(x, pltpu.HBM) for x in (assignment, database, queries, key_rows, hint)))

    placed = (P("col", "grp"), P("grp", "col"), P("grp", "col"), P("grp", None), P("grp"))
    return jax.shard_map(
        on_device,
        mesh=mesh,
        in_specs=placed,
        out_specs=P(("grp", "col"), None, None),
        check_vma=False,
    )
```

```python
import functools

import jax
import jax.numpy as jnp
from jax import lax
from jax.experimental import pallas as pl
from jax.experimental.pallas import tpu as pltpu
from jax.sharding import PartitionSpec as P

LEVELS = 2
DIGITS = 2
LANES = 128
WORD_BYTES = 4
DIGIT_BYTES = WORD_BYTES // DIGITS
SPAN = LANES // DIGIT_BYTES


def iota(shape, axis):
    return lax.broadcasted_iota(jnp.int32, shape, axis)


def byte_of(words, index):
    return jnp.bitwise_and(jnp.right_shift(words, 8 * index), 255).astype(jnp.float32)


def shifted(poly, amount):
    rows = poly.shape[0]
    amount = amount % (2 * rows * LANES)
    negate, turn = divmod(amount // LANES, rows)
    moved = poly
    if turn:
        moved = pltpu.roll(poly, turn, 0)
        moved = jnp.where(iota(poly.shape, 0) >= turn, moved, -moved)
    return -moved if negate else moved


def automorph(poly, level):
    step = poly.shape[0] * LANES >> level
    period = 2 << level
    residue = jnp.bitwise_and(iota(poly.shape, 1), period - 1)
    out = poly
    for m in range(1, period):
        out = jnp.where(residue == m, shifted(poly, step * m), out)
    return out


def fill_toeplitz(word_poly, toeplitz):
    rows = word_poly.shape[0]
    block = (SPAN, LANES)
    ahead = iota(block, 1) >= iota(block, 0)

    def turned(q):
        row = jnp.broadcast_to(word_poly[q : q + 1], block)
        return pltpu.roll(row, 0, 1, stride=1, stride_axis=0)

    before = turned(rows - 1)
    for q in range(rows):
        here = turned(q)
        words = jnp.where(ahead, here, before)
        for b in range(WORD_BYTES):
            part = byte_of(words, b)
            if q == 0:
                part = jnp.where(ahead, part, -part)
            toeplitz[b * SPAN : (b + 1) * SPAN, q * LANES : (q + 1) * LANES] = part.astype(
                jnp.bfloat16
            )
        before = here


def key_side(keys):
    owner = iota(keys[0][0].shape, 1) // SPAN
    zero = jnp.zeros(keys[0][0].shape, jnp.float32)
    blocks = []
    for s in range(WORD_BYTES):
        for p in range(2):
            for h in range(DIGIT_BYTES):
                tiles = []
                for t in range(DIGITS):
                    tile = zero
                    for a in range(min(s + 1, DIGIT_BYTES)):
                        part = byte_of(keys[t][p], s - a)
                        if a != h:
                            part = pltpu.roll(part, (a - h) % DIGIT_BYTES * SPAN, 1)
                        tile = jnp.where(owner == a, part, tile)
                    tiles.append(tile)
                blocks.append(jnp.concatenate(tiles, axis=1))
    return jnp.concatenate(blocks, axis=0).astype(jnp.bfloat16)


def switch(toeplitz, key_polys, rows):
    products = jnp.dot(
        key_side(key_polys), toeplitz[...], preferred_element_type=jnp.float32
    ).astype(jnp.int32)
    lane = iota((rows, LANES), 1)
    sums = []
    for p in range(2):
        total = jnp.zeros((rows, LANES), jnp.int32)
        for h in range(DIGIT_BYTES):
            words = None
            for s in range(WORD_BYTES):
                at = ((s * 2 + p) * DIGIT_BYTES + h) * rows
                term = jnp.left_shift(products[at : at + rows], 8 * s)
                words = term if words is None else words + term
            out = words[:, :LANES]
            for q in range(1, rows):
                out = out + shifted(words[:, q * LANES : (q + 1) * LANES], q * LANES)
            if h:
                turn = h * SPAN
                carried = pltpu.roll(shifted(out, LANES), turn, 1)
                out = jnp.where(lane >= turn, pltpu.roll(out, turn, 1), carried)
            total = total + out
        sums.append(total)
    return sums


def kernel(
    n, slots, share, assign_hbm, database_hbm, queries_hbm, keys_hbm, hint_hbm, out,
    assign, database, queries, keys, hint, loaded, part, unit_part, unit_keys, unit_masks, ans_send, key_send, ans_recv, key_recv, key_words, toeplitz,
    ans_sent, key_sent, ans_got, key_got,
):
    me = lax.axis_index("col")
    clients, columns = queries.shape
    polys, cycle = hint.shape
    rows = cycle // LANES
    key_rows = unit_keys.shape[1]
    barrier = pltpu.get_barrier_semaphore()

    def greet(i, carry):
        pl.semaphore_signal(barrier, inc=1, device_id={"col": lax.rem(me + i, n)})
        return carry

    lax.fori_loop(1, n, greet, 0)

    loads = [
        pltpu.make_async_copy(source, target, loaded.at[i])
        for i, (source, target) in enumerate(
            (
                (keys_hbm, keys),
                (hint_hbm, hint),
                (assign_hbm, assign),
                (queries_hbm, queries),
                (database_hbm, database),
            )
        )
    ]
    for load in loads:
        load.start()

    loads[0].wait()
    lane_owner = iota((clients, LANES), 1) // (LANES // share)
    for j in range(key_rows):
        tile = keys[:, j * LANES : (j + 1) * LANES]
        if share > 1:
            tile = jnp.where(lane_owner == lax.rem(me, share), tile, 0)
        for c in range(clients):
            for p in range(polys):
                unit_keys[c * polys + p, j : j + 1, :] = tile[c : c + 1]

    loads[1].wait()
    for p in range(polys):
        for q in range(rows):
            row = hint[p : p + 1, q * LANES : (q + 1) * LANES]
            for c in range(clients):
                unit_masks[c * polys + p, q : q + 1, :] = row

    for load in loads[2:]:
        load.wait()
    query_words = queries[...]
    query_bytes = jnp.concatenate([byte_of(query_words, b) for b in range(WORD_BYTES)], axis=0)
    products = jnp.dot(
        query_bytes.astype(jnp.bfloat16),
        database[...].astype(jnp.float32).astype(jnp.bfloat16),
        preferred_element_type=jnp.float32,
    ).astype(jnp.int32)
    partial = products[:clients]
    for b in range(1, WORD_BYTES):
        partial = partial + jnp.left_shift(products[b * clients : (b + 1) * clients], 8 * b)
    for j in range(polys * rows):
        part[j * clients : (j + 1) * clients, :] = partial[:, j * LANES : (j + 1) * LANES]

    for c in range(clients):
        for p in range(polys):
            unit_part[c * polys + p] = part[pl.ds(p * rows * clients + c, rows, stride=clients), :]

    def stage_into(ans, key, at, owner):
        for k in range(slots):
            unit = assign[owner * slots + k]
            ans[at, k * rows : (k + 1) * rows, :] = unit_part[unit]
            key[at, k * key_rows : (k + 1) * key_rows, :] = unit_keys[unit]

    def stage(i, carry):
        owner = lax.rem(me + i, n)
        stage_into(ans_send, key_send, owner, owner)
        return carry

    lax.fori_loop(1, n, stage, 0)
    stage_into(ans_recv, key_recv, me, me)

    pl.semaphore_wait(barrier, n - 1)

    def remote(source, target, there, sent, got):
        return pltpu.make_async_remote_copy(
            src_ref=source.at[there],
            dst_ref=target.at[me],
            send_sem=sent,
            recv_sem=got,
            device_id={"col": there},
        )

    def send_keys(i, carry):
        remote(key_send, key_recv, lax.rem(me + i, n), key_sent, key_got).start()
        return carry

    def send_answers(i, carry):
        remote(ans_send, ans_recv, lax.rem(me + i, n), ans_sent, ans_got).start()
        return carry

    def wait_all(buffer, semaphore):
        blocks = buffer.at[pl.ds(0, n - 1)]
        pltpu.make_async_copy(blocks, blocks, semaphore).wait()

    lax.fori_loop(1, n, send_keys, 0)
    lax.fori_loop(1, n, send_answers, 0)

    switched = []
    for k in range(slots):
        mask = unit_masks[assign[me * slots + k]]
        fill_toeplitz(automorph(mask, 0), toeplitz)
        if k == 0:
            wait_all(key_recv, key_got)
        for j in range(n // share):
            block = key_recv[j * share, k * key_rows : (k + 1) * key_rows, :]
            for h in range(1, share):
                block = block + key_recv[j * share + h, k * key_rows : (k + 1) * key_rows, :]
            key_words[j * key_rows : (j + 1) * key_rows, :] = block
        added = []
        for level in range(LEVELS):
            if level:
                fill_toeplitz(automorph(mask, level), toeplitz)

            def key_poly(t, p):
                at = ((level * DIGITS + t) * 2 + p) * rows
                return key_words[at : at + rows, :]

            to_mask, to_value = switch(
                toeplitz, [[key_poly(t, p) for p in range(2)] for t in range(DIGITS)], rows
            )
            mask = mask + to_mask
            added.append(to_value)
        switched.append((mask, added))

    wait_all(ans_recv, ans_got)
    for k, (mask, added) in enumerate(switched):
        value = ans_recv[0, k * rows : (k + 1) * rows, :]
        for j in range(1, n):
            value = value + ans_recv[j, k * rows : (k + 1) * rows, :]
        for level in range(LEVELS):
            value = value + automorph(value, level) + added[level]
        for index, words in enumerate((mask, value)):
            scaled = words.astype(jnp.float32) * 2.0 ** (-32)
            for q in range(rows):
                out[k, index : index + 1, q * LANES : (q + 1) * LANES] = scaled[q : q + 1]
    wait_all(key_send, key_sent)
    wait_all(ans_send, ans_sent)


def solution(mesh):
    n = mesh.shape["col"]

    def on_device(database, queries, key_rows, hint, assignment):
        clients = queries.shape[0]
        polys, cycle = hint.shape
        rows = cycle // LANES
        slots = assignment.shape[0] // n
        width = key_rows.shape[1]
        share = max(1, LANES // width)
        if share > 1:
            key_rows = jnp.tile(key_rows, (1, share))
        tiles = key_rows.shape[1] // LANES
        place = pl.BlockSpec(memory_space=pltpu.HBM)
        return pl.pallas_call(
            functools.partial(kernel, n, slots, share),
            out_shape=pltpu.VMEM((slots, 2, cycle), jnp.float32),
            in_specs=[place] * 5,
            out_specs=pl.BlockSpec(memory_space=pltpu.VMEM),
            scratch_shapes=[
                pltpu.SMEM(assignment.shape, jnp.int32),
                pltpu.VMEM(database.shape, jnp.int32),
                pltpu.VMEM(queries.shape, jnp.int32),
                pltpu.VMEM(key_rows.shape, jnp.int32),
                pltpu.VMEM(hint.shape, jnp.int32),
                pltpu.SemaphoreType.DMA((5,)),
                pltpu.VMEM((polys * rows * clients, LANES), jnp.int32),
                pltpu.VMEM((polys * clients, rows, LANES), jnp.int32),
                pltpu.VMEM((polys * clients, tiles, LANES), jnp.int32),
                pltpu.VMEM((polys * clients, rows, LANES), jnp.int32),
                pltpu.VMEM((n, slots * rows, LANES), jnp.int32),
                pltpu.VMEM((n, slots * tiles, LANES), jnp.int32),
                pltpu.VMEM((n, slots * rows, LANES), jnp.int32),
                pltpu.VMEM((n, slots * tiles, LANES), jnp.int32),
                pltpu.VMEM((n // share * tiles, LANES), jnp.int32),
                pltpu.VMEM((WORD_BYTES * SPAN, cycle), jnp.bfloat16),
                pltpu.SemaphoreType.DMA,
                pltpu.SemaphoreType.DMA,
                pltpu.SemaphoreType.DMA,
                pltpu.SemaphoreType.DMA,
            ],
            compiler_params=pltpu.CompilerParams(
                collective_id=0, has_side_effects=True
            ),
        )(*(pltpu.with_memory_space_constraint(x, pltpu.HBM) for x in (assignment, database, queries, key_rows, hint)))

    placed = (P("col", "grp"), P("grp", "col"), P("grp", "col"), P("grp", None), P("grp"))
    return jax.shard_map(
        on_device,
        mesh=mesh,
        in_specs=placed,
        out_specs=P(("grp", "col"), None, None),
        check_vma=False,
    )
```

```python
import functools

import jax
import jax.numpy as jnp
from jax import lax
from jax.experimental import pallas as pl
from jax.experimental.pallas import tpu as pltpu
from jax.sharding import PartitionSpec as P

LEVELS = 2
DIGITS = 2
LANES = 128
WORD_BYTES = 4
DIGIT_BYTES = WORD_BYTES // DIGITS
SPAN = LANES // DIGIT_BYTES


def iota(shape, axis):
    return lax.broadcasted_iota(jnp.int32, shape, axis)


def byte_of(words, index):
    return jnp.bitwise_and(jnp.right_shift(words, 8 * index), 255).astype(jnp.float32)


def shifted(poly, amount):
    rows = poly.shape[0]
    amount = amount % (2 * rows * LANES)
    negate, turn = divmod(amount // LANES, rows)
    moved = poly
    if turn:
        moved = pltpu.roll(poly, turn, 0)
        moved = jnp.where(iota(poly.shape, 0) >= turn, moved, -moved)
    return -moved if negate else moved


def automorph(poly, level):
    step = poly.shape[0] * LANES >> level
    period = 2 << level
    residue = jnp.bitwise_and(iota(poly.shape, 1), period - 1)
    out = poly
    for m in range(1, period):
        out = jnp.where(residue == m, shifted(poly, step * m), out)
    return out


def fill_toeplitz(word_poly, toeplitz):
    rows = word_poly.shape[0]
    block = (SPAN, LANES)
    ahead = iota(block, 1) >= iota(block, 0)

    def turned(q):
        row = jnp.broadcast_to(word_poly[q : q + 1], block)
        return pltpu.roll(row, 0, 1, stride=1, stride_axis=0)

    before = turned(rows - 1)
    for q in range(rows):
        here = turned(q)
        words = jnp.where(ahead, here, before)
        for b in range(WORD_BYTES):
            part = byte_of(words, b)
            if q == 0:
                part = jnp.where(ahead, part, -part)
            toeplitz[b * SPAN : (b + 1) * SPAN, q * LANES : (q + 1) * LANES] = part.astype(
                jnp.bfloat16
            )
        before = here


def key_side(keys):
    owner = iota(keys[0][0].shape, 1) // SPAN
    zero = jnp.zeros(keys[0][0].shape, jnp.float32)
    blocks = []
    for s in range(WORD_BYTES):
        for p in range(2):
            for h in range(DIGIT_BYTES):
                tiles = []
                for t in range(DIGITS):
                    tile = zero
                    for a in range(min(s + 1, DIGIT_BYTES)):
                        part = byte_of(keys[t][p], s - a)
                        if a != h:
                            part = pltpu.roll(part, (a - h) % DIGIT_BYTES * SPAN, 1)
                        tile = jnp.where(owner == a, part, tile)
                    tiles.append(tile)
                blocks.append(jnp.concatenate(tiles, axis=1))
    return jnp.concatenate(blocks, axis=0).astype(jnp.bfloat16)


def switch(toeplitz, key_polys, rows):
    products = jnp.dot(
        key_side(key_polys), toeplitz[...], preferred_element_type=jnp.float32
    ).astype(jnp.int32)
    lane = iota((rows, LANES), 1)
    sums = []
    for p in range(2):
        total = jnp.zeros((rows, LANES), jnp.int32)
        for h in range(DIGIT_BYTES):
            words = None
            for s in range(WORD_BYTES):
                at = ((s * 2 + p) * DIGIT_BYTES + h) * rows
                term = jnp.left_shift(products[at : at + rows], 8 * s)
                words = term if words is None else words + term
            out = words[:, :LANES]
            for q in range(1, rows):
                out = out + shifted(words[:, q * LANES : (q + 1) * LANES], q * LANES)
            if h:
                turn = h * SPAN
                carried = pltpu.roll(shifted(out, LANES), turn, 1)
                out = jnp.where(lane >= turn, pltpu.roll(out, turn, 1), carried)
            total = total + out
        sums.append(total)
    return sums


def kernel(
    n, slots, share, assign_hbm, database_hbm, queries_hbm, keys_hbm, hint_hbm, out,
    assign, database, queries, keys, hint, loaded, part, unit_part, unit_keys, unit_masks, ans_send, key_send, ans_recv, key_recv, key_words, toeplitz,
    ans_sent, key_sent, ans_got, key_got,
):
    me = lax.axis_index("col")
    clients, columns = queries.shape
    polys, cycle = hint.shape
    rows = cycle // LANES
    key_rows = unit_keys.shape[1]
    barrier = pltpu.get_barrier_semaphore()

    def greet(i, carry):
        pl.semaphore_signal(barrier, inc=1, device_id={"col": lax.rem(me + i, n)})
        return carry

    lax.fori_loop(1, n, greet, 0, unroll=n <= LANES // 8)

    loads = [
        pltpu.make_async_copy(source, target, loaded.at[i])
        for i, (source, target) in enumerate(
            (
                (keys_hbm, keys),
                (hint_hbm, hint),
                (assign_hbm, assign),
                (queries_hbm, queries),
                (database_hbm, database),
            )
        )
    ]
    for load in loads:
        load.start()

    loads[0].wait()
    lane_owner = iota((clients, LANES), 1) // (LANES // share)
    for j in range(key_rows):
        tile = keys[:, j * LANES : (j + 1) * LANES]
        if share > 1:
            tile = jnp.where(lane_owner == lax.rem(me, share), tile, 0)
        for c in range(clients):
            for p in range(polys):
                unit_keys[c * polys + p, j : j + 1, :] = tile[c : c + 1]

    loads[1].wait()
    for p in range(polys):
        for q in range(rows):
            row = hint[p : p + 1, q * LANES : (q + 1) * LANES]
            for c in range(clients):
                unit_masks[c * polys + p, q : q + 1, :] = row

    for load in loads[2:]:
        load.wait()
    query_words = queries[...]
    query_bytes = jnp.concatenate([byte_of(query_words, b) for b in range(WORD_BYTES)], axis=0)
    products = jnp.dot(
        query_bytes.astype(jnp.bfloat16),
        database[...].astype(jnp.float32).astype(jnp.bfloat16),
        preferred_element_type=jnp.float32,
    ).astype(jnp.int32)
    partial = products[:clients]
    for b in range(1, WORD_BYTES):
        partial = partial + jnp.left_shift(products[b * clients : (b + 1) * clients], 8 * b)
    for j in range(polys * rows):
        part[j * clients : (j + 1) * clients, :] = partial[:, j * LANES : (j + 1) * LANES]

    for c in range(clients):
        for p in range(polys):
            unit_part[c * polys + p] = part[pl.ds(p * rows * clients + c, rows, stride=clients), :]

    def stage_into(ans, key, at, owner):
        for k in range(slots):
            unit = assign[owner * slots + k]
            ans[at, k * rows : (k + 1) * rows, :] = unit_part[unit]
            key[at, k * key_rows : (k + 1) * key_rows, :] = unit_keys[unit]

    def stage(i, carry):
        owner = lax.rem(me + i, n)
        stage_into(ans_send, key_send, owner, owner)
        return carry

    lax.fori_loop(1, n, stage, 0)
    stage_into(ans_recv, key_recv, me, me)

    pl.semaphore_wait(barrier, n - 1)

    def remote(source, target, there, sent, got):
        return pltpu.make_async_remote_copy(
            src_ref=source.at[there],
            dst_ref=target.at[me],
            send_sem=sent,
            recv_sem=got,
            device_id={"col": there},
        )

    def send_keys(i, carry):
        remote(key_send, key_recv, lax.rem(me + i, n), key_sent, key_got).start()
        return carry

    def send_answers(i, carry):
        remote(ans_send, ans_recv, lax.rem(me + i, n), ans_sent, ans_got).start()
        return carry

    def wait_all(buffer, semaphore):
        blocks = buffer.at[pl.ds(0, n - 1)]
        pltpu.make_async_copy(blocks, blocks, semaphore).wait()

    lax.fori_loop(1, n, send_keys, 0, unroll=n <= LANES // 8)
    lax.fori_loop(1, n, send_answers, 0)

    switched = []
    for k in range(slots):
        mask = unit_masks[assign[me * slots + k]]
        fill_toeplitz(automorph(mask, 0), toeplitz)
        if k == 0:
            wait_all(key_recv, key_got)
        for j in range(n // share):
            block = key_recv[j * share, k * key_rows : (k + 1) * key_rows, :]
            for h in range(1, share):
                block = block + key_recv[j * share + h, k * key_rows : (k + 1) * key_rows, :]
            key_words[j * key_rows : (j + 1) * key_rows, :] = block
        added = []
        for level in range(LEVELS):
            if level:
                fill_toeplitz(automorph(mask, level), toeplitz)

            def key_poly(t, p):
                at = ((level * DIGITS + t) * 2 + p) * rows
                return key_words[at : at + rows, :]

            to_mask, to_value = switch(
                toeplitz, [[key_poly(t, p) for p in range(2)] for t in range(DIGITS)], rows
            )
            mask = mask + to_mask
            added.append(to_value)
        switched.append((mask, added))

    wait_all(ans_recv, ans_got)
    for k, (mask, added) in enumerate(switched):
        value = ans_recv[0, k * rows : (k + 1) * rows, :]
        for j in range(1, n):
            value = value + ans_recv[j, k * rows : (k + 1) * rows, :]
        for level in range(LEVELS):
            value = value + automorph(value, level) + added[level]
        for index, words in enumerate((mask, value)):
            scaled = words.astype(jnp.float32) * 2.0 ** (-32)
            for q in range(rows):
                out[k, index : index + 1, q * LANES : (q + 1) * LANES] = scaled[q : q + 1]
    wait_all(key_send, key_sent)
    wait_all(ans_send, ans_sent)


def solution(mesh):
    n = mesh.shape["col"]

    def on_device(database, queries, key_rows, hint, assignment):
        clients = queries.shape[0]
        polys, cycle = hint.shape
        rows = cycle // LANES
        slots = assignment.shape[0] // n
        width = key_rows.shape[1]
        share = max(1, LANES // width)
        if share > 1:
            key_rows = jnp.tile(key_rows, (1, share))
        tiles = key_rows.shape[1] // LANES
        place = pl.BlockSpec(memory_space=pltpu.HBM)
        return pl.pallas_call(
            functools.partial(kernel, n, slots, share),
            out_shape=pltpu.VMEM((slots, 2, cycle), jnp.float32),
            in_specs=[place] * 5,
            out_specs=pl.BlockSpec(memory_space=pltpu.VMEM),
            scratch_shapes=[
                pltpu.SMEM(assignment.shape, jnp.int32),
                pltpu.VMEM(database.shape, jnp.int32),
                pltpu.VMEM(queries.shape, jnp.int32),
                pltpu.VMEM(key_rows.shape, jnp.int32),
                pltpu.VMEM(hint.shape, jnp.int32),
                pltpu.SemaphoreType.DMA((5,)),
                pltpu.VMEM((polys * rows * clients, LANES), jnp.int32),
                pltpu.VMEM((polys * clients, rows, LANES), jnp.int32),
                pltpu.VMEM((polys * clients, tiles, LANES), jnp.int32),
                pltpu.VMEM((polys * clients, rows, LANES), jnp.int32),
                pltpu.VMEM((n, slots * rows, LANES), jnp.int32),
                pltpu.VMEM((n, slots * tiles, LANES), jnp.int32),
                pltpu.VMEM((n, slots * rows, LANES), jnp.int32),
                pltpu.VMEM((n, slots * tiles, LANES), jnp.int32),
                pltpu.VMEM((n // share * tiles, LANES), jnp.int32),
                pltpu.VMEM((WORD_BYTES * SPAN, cycle), jnp.bfloat16),
                pltpu.SemaphoreType.DMA,
                pltpu.SemaphoreType.DMA,
                pltpu.SemaphoreType.DMA,
                pltpu.SemaphoreType.DMA,
            ],
            compiler_params=pltpu.CompilerParams(
                collective_id=0, has_side_effects=True
            ),
        )(*(pltpu.with_memory_space_constraint(x, pltpu.HBM) for x in (assignment, database, queries, key_rows, hint)))

    placed = (P("col", "grp"), P("grp", "col"), P("grp", "col"), P("grp", None), P("grp"))
    return jax.shard_map(
        on_device,
        mesh=mesh,
        in_specs=placed,
        out_specs=P(("grp", "col"), None, None),
        check_vma=False,
    )
```
